32 devices in a mesh: tm: 16 (over z, x, core), space: 2 (over y).
Axes of the slice: x: 2, y: 2, z: 4, core: 2. Of those that a mesh axis runs over, the one named last changes fastest.
Arguments:
- nodes: float32 [16, 2, 2, 8, 128, 128], P('tm', None, None, 'space'), may hold values from -3 to 3
- initial: float32 [2, 8, 128, 128], P(None, 'space'), may hold values from -3 to 3
Outputs:
- corrected: float32 [16, 2, 2, 8, 128, 128], P('tm', None, None, 'space')
The draws below stay inside these ranges and needn't reach their ends.
All inputs are finite; a program needn't handle non-finite values.
Results may differ from the reference program's by a relative error of at most 0.0003.
Values sent between devices are 32-bit elements; how exact they have to be, the bound alone decides.
No kernel may reach another device: no remote copies, remote signals or barrier semaphores. Data moves between devices by JAX's collectives and lax.ppermute only.
A program may use at most 128 MiB of HBM per device.

```python
import math
import jax
import jax.numpy as jnp
from jax import lax

NX = 128
NY = 128
SLICES = 16
NZ = 8


def level_of(rng, shape, shards, least, largest):
    loudness = 1.0
    for dim, parts in shards:
        heights = jax.random.uniform(jax.random.fold_in(jax.random.fold_in(rng, 6), dim), (parts,), jnp.float32, least / len(shards), largest / len(shards))
        loudness = loudness * jnp.repeat(jnp.exp(heights), shape[dim] // parts).reshape((-1,) + (1,) * (len(shape) - 1 - dim))
    return loudness


def centred(key, dims, deviation, most, pieces=(), dtype=jnp.bfloat16):
    result = deviation * jax.random.normal(key, dims, jnp.float32)
    if pieces:
        result = result * level_of(key, dims, pieces, -0.22, 0.18)
    return jnp.clip(result, -most, most).astype(dtype)


def setup_inputs(seed: int = 0) -> dict:
    streams_of = jax.random.split(jax.random.key(seed), 3)
    return {
        "nodes": centred(streams_of[0], (SLICES, 2, 2, NZ, NX, NY), 0.5, 3.0, ((0, 16), (3, 2)), jnp.float32),
        "initial": centred(streams_of[1], (2, NZ, NX, NY), 0.5, 3.0, ((1, 2),), jnp.float32),
    }


diffuse_fast = 0.5
diffuse_slow = 0.25
feed_rate = 0.04
kill_rate = 0.06
slice_length = 0.5
node_step = 0.25
sweep_weights = ((5.0 / 24.0, 1.0 / 3.0, -1.0 / 24.0), (-1.0 / 24.0, 1.0 / 3.0, 5.0 / 24.0))

def sine_table(points, modes, stretch):
    place = jnp.arange(points).astype(jnp.float32) + 0.5
    order = jnp.arange(modes).astype(jnp.float32) + 1.0
    angle = math.pi / (stretch * modes) * place[:, None] * order[None, :]
    weight = jnp.where(jnp.arange(modes) == modes - 1, math.sqrt(0.5), 1.0).astype(jnp.float32)
    return math.sqrt(2.0 / modes) * weight[None, :] * jnp.sin(angle)

def eigenvalues(count):
    order = jnp.arange(count).astype(jnp.float32) + 1.0
    return 2.0 * jnp.cos(math.pi * order / count) - 2.0

def tendency(values):
    center = values[..., 1:-1, :, :]
    padded = jnp.pad(center, [(0, 0)] * (center.ndim - 2) + [(1, 1), (1, 1)])
    laplace = values[..., 2:, :, :] + values[..., :-2, :, :] + padded[..., 2:, 1:-1] + padded[..., :-2, 1:-1]
    laplace = laplace + padded[..., 1:-1, 2:] + padded[..., 1:-1, :-2] - 6.0 * center
    first_kind = center[..., 0, :, :, :]
    second_kind = center[..., 1, :, :, :]
    reaction = (1.0 + first_kind) * second_kind * second_kind
    first_rate = diffuse_fast * laplace[..., 0, :, :, :] - reaction - feed_rate * first_kind
    second_rate = diffuse_slow * laplace[..., 1, :, :, :] + reaction - (feed_rate + kill_rate) * second_kind
    return jnp.stack([first_rate, second_rate], axis=-4)

def restrict(values):
    shape = values.shape
    blocks = values.reshape(shape[:-3] + (shape[-3] // 2, 2, shape[-2] // 2, 2, shape[-1] // 2, 2))
    return lax.optimization_barrier(jnp.mean(blocks, axis=(-5, -3, -1)))

def reference(nodes, initial):
    modes_x = NX // 2
    modes_y = NY // 2
    modes_z = NZ // 2
    forward_x = sine_table(modes_x, modes_x, 1.0).T
    forward_y = sine_table(modes_y, modes_y, 1.0).T
    forward_z = sine_table(modes_z, modes_z, 1.0).T
    interp_x = sine_table(NX, modes_x, 2.0)
    interp_y = sine_table(NY, modes_y, 2.0)
    interp_z = sine_table(NZ, modes_z, 2.0)
    eigen_sum = (eigenvalues(modes_z)[:, None, None] + eigenvalues(modes_x)[None, :, None] + eigenvalues(modes_y)[None, None, :]) / 4.0
    linear = jnp.stack([diffuse_fast * eigen_sum - feed_rate, diffuse_slow * eigen_sum - (feed_rate + kill_rate)])
    factor = 1.0 / (1.0 - node_step * linear)
    highest = lax.Precision.HIGHEST

    def widen(values):
        return jnp.pad(values, ((0, 0), (1, 1), (0, 0), (0, 0)))

    def forward(values):
        step_y = jnp.einsum('by,szxy->szxb', forward_y, values, precision=highest)
        step_x = jnp.einsum('ax,szxb->szab', forward_x, step_y, precision=highest)
        return jnp.einsum('kz,szab->skab', forward_z, step_x, precision=highest)

    def backward(spectra):
        step_z = jnp.einsum('zk,skab->szab', interp_z, spectra, precision=highest)
        step_y = jnp.einsum('yb,szab->szay', interp_y, step_z, precision=highest)
        return jnp.einsum('xa,szay->szxy', interp_x, step_y, precision=highest)
    (w00, w01, w02), (w10, w11, w12) = sweep_weights

    def advance(carry, inputs):
        prior_end, chain = carry
        own_nodes, position = inputs
        start_value = jnp.where(position == 0, initial, prior_end)
        middle = own_nodes[0]
        finish = own_nodes[1]
        slope_zero = tendency(widen(start_value))
        slope_mid = tendency(widen(middle))
        slope_end = tendency(widen(finish))
        swept_one = start_value + slice_length * (w00 * slope_zero + w01 * slope_mid + w02 * slope_end)
        slope_one = tendency(widen(swept_one))
        swept_two = swept_one + node_step * (slope_one - slope_mid) + slice_length * (w10 * slope_zero + w11 * slope_mid + w12 * slope_end)
        slope_two = tendency(widen(swept_two))
        integral_one = slice_length * (w00 * slope_zero + w01 * slope_one + w02 * slope_two)
        integral_two = slice_length * (w10 * slope_zero + w11 * slope_one + w12 * slope_two)
        quad_one = forward(restrict(integral_one))
        quad_two = forward(restrict(integral_two))
        coarse_zero = forward(restrict(start_value))
        coarse_one = forward(restrict(swept_one))
        coarse_two = forward(restrict(swept_two))
        remain_one = quad_one - node_step * linear * coarse_one
        remain_two = quad_two - node_step * linear * coarse_two
        start_hat = jnp.where(position == 0, coarse_zero, chain)
        new_one = factor * (start_hat + remain_one)
        new_two = factor * (new_one + remain_two)
        out_one = swept_one + backward(new_one - coarse_one)
        out_two = swept_two + backward(new_two - coarse_two)
        return ((finish, new_two), jnp.stack([out_one, out_two]))
    empty = jnp.zeros((2, modes_z, modes_x, modes_y), jnp.float32)
    positions = jnp.arange(SLICES).astype(jnp.int32)
    _, corrected = lax.scan(advance, (initial, empty), (nodes, positions))
    return corrected
```

```python
import functools
import math

import jax
import jax.numpy as jnp
import numpy as np
from jax import lax
from jax.experimental import pallas as pl
from jax.experimental.pallas import tpu as pltpu
from jax.sharding import PartitionSpec as P

diffusion = (0.5, 0.25)
feed_rate = 0.04
kill_rate = 0.06
decay = (feed_rate, feed_rate + kill_rate)
slice_length = 0.5
node_step = 0.25
sweep_weights = ((5.0 / 24.0, 1.0 / 3.0, -1.0 / 24.0), (-1.0 / 24.0, 1.0 / 3.0, 5.0 / 24.0))
(T00, T01, T02), (T10, T11, T12) = [[slice_length * w for w in row] for row in sweep_weights]
AXES = ("tm", "space")


def sine_table(points, modes):
    place = np.arange(points) + 0.5
    order = np.arange(modes) + 1.0
    weight = np.where(np.arange(modes) == modes - 1, math.sqrt(0.5), 1.0)
    return math.sqrt(2.0 / modes) * weight[None, :] * np.sin(math.pi / points * place[:, None] * order[None, :])


def split(table):
    table = jnp.asarray(table, jnp.float32)
    high = table.astype(jnp.bfloat16)
    low = (table - high.astype(jnp.float32)).astype(jnp.bfloat16)
    return high, low


def np_split(table):
    table = np.asarray(table, np.float32)
    high = table.astype(jnp.bfloat16)
    low = (table - high.astype(np.float32)).astype(jnp.bfloat16)
    return high, low


def restricted(modes):
    return np.repeat(sine_table(modes, modes).T, 2, axis=1) * 0.5


def doubled(table):
    rows, columns = table.shape
    both = np.zeros((2 * rows, 2 * columns))
    both[:rows, :columns] = table
    both[rows:, columns:] = table
    return both


def eigen(count):
    return 2.0 * np.cos(math.pi * (np.arange(count) + 1.0) / count) - 2.0


def factor_table(modes_z, modes_x, modes_y):
    total = (eigen(modes_z)[:, None, None] + eigen(modes_x)[None, :, None] + eigen(modes_y)[None, None, :]) / 4.0
    linear = np.stack([diffusion[i] * total - decay[i] for i in range(2)], axis=2)
    factor = 1.0 / (1.0 - node_step * linear)
    return np.asarray(factor.reshape(modes_z * modes_x, 2 * modes_y), np.float32)


def in_plane(v):
    rows, lanes = v.shape
    row = lax.broadcasted_iota(jnp.int32, v.shape, 0)
    lane = lax.broadcasted_iota(jnp.int32, v.shape, 1)
    up = jnp.where(row == rows - 1, 0.0, pltpu.roll(v, rows - 1, 0))
    down = jnp.where(row == 0, 0.0, pltpu.roll(v, 1, 0))
    left = jnp.where(lane == lanes - 1, 0.0, pltpu.roll(v, lanes - 1, 1))
    right = jnp.where(lane == 0, 0.0, pltpu.roll(v, 1, 1))
    return (up + down) + (left + right)


def slopes(p, q, beside_p, beside_q):
    lap_p = in_plane(p) + beside_p - 6.0 * p
    lap_q = in_plane(q) + beside_q - 6.0 * q
    reaction = (1.0 + p) * q * q
    return (
        diffusion[0] * lap_p - reaction - decay[0] * p,
        diffusion[1] * lap_q + reaction - decay[1] * q,
    )


def dot(a, b):
    return jnp.dot(a, b, preferred_element_type=jnp.float32)


def edge_plane(side, planes, inward):
    if isinstance(side, int):
        return inward if side == 0 else planes - 1 - inward
    return jnp.where(side == 0, inward, planes - 1 - inward)


def facing(spaces):
    if spaces == 2:
        return [1 - lax.axis_index("space")]
    return [0, 1]


def prepare_kernel(spaces, count, nodes, initial, finish, *outs):
    planes = nodes.shape[3]
    is_last = lax.axis_index("tm") == count - 1
    finish[...] = nodes[0, 1]
    for n, side in enumerate(facing(spaces)):
        own, diagonal = outs[2 * n], outs[2 * n + 1]
        first, second = edge_plane(side, planes, 0), edge_plane(side, planes, 1)

        def at(node, plane):
            return [nodes[0, node, s, plane] for s in range(2)]

        mid, end = at(0, first), at(1, first)
        mid_slope = slopes(*mid, *at(0, second))
        end_slope = slopes(*end, *at(1, second))
        start = [jnp.where(is_last, initial[s, first], end[s]) for s in range(2)]
        beside = [jnp.where(is_last, initial[s, second], nodes[0, 1, s, second]) for s in range(2)]
        start_slope = slopes(*start, *beside)
        for s in range(2):
            own[0, s] = T01 * mid[s] + T02 * end[s]
            own[1, s] = (
                node_step * (T01 * mid_slope[s] + T02 * end_slope[s])
                + (T11 - node_step) * mid[s]
                + T12 * end[s]
            )
            diagonal[0, s] = start[s]
            diagonal[1, s] = node_step * (start[s] + T00 * start_slope[s]) + T10 * start[s]


def sweep_kernel(spaces, *refs):
    refs = list(refs)
    table_z, interp_z = refs.pop(0), refs.pop(0)
    nodes, initial, prior = refs.pop(0), refs.pop(0), refs.pop(0)
    halos = [(refs.pop(0), refs.pop(0)) for _ in range(1 if spaces == 2 else 2)]
    table_x, table_y, table_f = refs.pop(0), refs.pop(0), refs.pop(0)
    swept, element, keep = refs.pop(0), refs.pop(0), refs.pop(0)
    sends = [refs.pop(0) for _ in range(spaces - 1)]
    start, slope0, rest, xs, ys, stack, spec = refs
    planes = nodes.shape[3]
    half = planes // 2
    modes_x = table_x.shape[1]
    modes_z = table_f.shape[0] // modes_x
    lanes = table_f.shape[1]
    me = lax.axis_index("space")
    is_first = lax.axis_index("tm") == 0
    sides = facing(spaces)

    def beside(get, plane):
        around = [get(z) for z in (plane - 1, plane + 1) if 0 <= z < planes]
        return around[0] if len(around) == 1 else around[0] + around[1]

    def slope_of(ref, plane):
        args = [ref[s, plane] for s in range(2)] + [beside(lambda z: ref[s, z], plane) for s in range(2)]
        return slopes(*args)

    for z in range(planes):
        for s in range(2):
            start[s, z] = jnp.where(is_first, initial[s, z], prior[s, z])
    middle, finish = nodes.at[0, 0], nodes.at[0, 1]
    one, two = swept.at[0], swept.at[1]
    for z in range(planes):
        f0, f1, f2 = slope_of(start, z), slope_of(middle, z), slope_of(finish, z)
        for s in range(2):
            one[s, z] = start[s, z] + T00 * f0[s] + T01 * f1[s] + T02 * f2[s]
            rest[s, z] = T10 * f0[s] + (T11 - node_step) * f1[s] + T12 * f2[s]
            slope0[s, z] = f0[s]
    for side, (own, diagonal) in zip(sides, halos):
        edge = edge_plane(side, planes, 0)
        for s in range(2):
            d = diffusion[s]
            one[s, edge] = one[s, edge] + d * (T00 * diagonal[0, s] + own[0, s])
            back = T00 * start[s, edge] + T01 * middle[s, edge] + T02 * finish[s, edge]
            if spaces != 2:
                back = jnp.where(me == (0 if side == 0 else spaces - 1), 0.0, back)
            rest[s, edge] = rest[s, edge] + d * (own[1, s] + diagonal[1, s] + (node_step * d) * back)
    for z in range(planes):
        g1 = slope_of(one, z)
        for s in range(2):
            first = one[s, z]
            second = first + node_step * g1[s] + rest[s, z]
            two[s, z] = second
            x = T00 * slope0[s, z] + T01 * g1[s] - first
            xs[s, z] = x + jnp.where(is_first, start[s, z], 0.0)
            ys[s, z] = T10 * slope0[s, z] + T11 * g1[s] + first - second
    width_y = nodes.shape[5]
    rows = nodes.shape[4]

    def put(slot, s, value):
        stack[pl.ds(slot * rows, rows), pl.ds(s * width_y, width_y)] = value

    for c in range(half):
        pair = [slope_of(two, 2 * c), slope_of(two, 2 * c + 1)]
        for s in range(2):
            g2 = pair[0][s] + pair[1][s]
            put(c, s, 0.5 * (xs[s, 2 * c] + xs[s, 2 * c + 1] + T02 * g2))
            put(half + c, s, 0.5 * (ys[s, 2 * c] + ys[s, 2 * c + 1] + T12 * g2))
            put(2 * half + c, s, 0.5 * (two[s, 2 * c] + two[s, 2 * c + 1]))
    for n, side in enumerate(sides):
        edge = edge_plane(side, planes, 0)
        for s in range(2):
            d = 0.5 * diffusion[s]
            put(3 * half + 2 * n, s, d * (T00 * start[s, edge] + T01 * one[s, edge] + T02 * two[s, edge]))
            put(3 * half + 2 * n + 1, s, d * (T10 * start[s, edge] + T11 * one[s, edge] + T12 * two[s, edge]))
    fields = 3 * half + 2 * len(sides)
    y_high, y_low = table_y[0], table_y[1]
    x_high, x_low = table_x[0], table_x[1]
    for f in range(fields):
        high, low = split(stack[pl.ds(f * rows, rows), :])
        along_y = dot(high, y_high) + (dot(low, y_high) + dot(high, y_low))
        high, low = split(along_y)
        spec[f] = dot(x_high, high) + (dot(x_low, high) + dot(x_high, low))

    x_parts, y_parts = [], []
    for k in range(modes_z):
        factor = table_f[pl.ds(k * modes_x, modes_x), :]
        weights = [table_z[k, me * half + c] for c in range(half)]
        x = sum(weights[c] * spec[c] for c in range(half))
        y = sum(weights[c] * spec[half + c] for c in range(half))
        e = sum(weights[c] * spec[2 * half + c] for c in range(half))
        for n, side in enumerate(sides):
            beyond = me * half + jnp.where(side == 0, -1, half)
            inside = (beyond >= 0) & (beyond < spaces * half)
            weight = jnp.where(inside, table_z[k, jnp.clip(beyond, 0, spaces * half - 1)], 0.0)
            x = x + weight * spec[3 * half + 2 * n]
            y = y + weight * spec[3 * half + 2 * n + 1]
        x = factor * x
        y = factor * (x + y)
        element[pl.ds(k * modes_x, modes_x), :] = y + e
        x_parts.append(x)
        y_parts.append(y)
    for j, target in enumerate([keep] + sends):
        device = lax.rem(me + j, spaces)
        for z in range(planes):
            place = device * planes + z
            weights = [interp_z[place, k] for k in range(modes_z)]
            target[0, z] = sum(w * v for w, v in zip(weights, x_parts))
            target[1, z] = sum(w * v for w, v in zip(weights, y_parts))


def chain_kernel(count, spaces, pieces, factor, out):
    gain = factor[...] * factor[...]
    state = jnp.zeros_like(gain)
    for t in range(count):
        for s in range(spaces):
            out[t * spaces + s] = state
        if t < count - 1:
            total = pieces[t * spaces]
            for s in range(1, spaces):
                total = total + pieces[t * spaces + s]
            state = gain * state + total


def finish_kernel(spaces, interp_z, carried, swept, keep, *refs):
    received = refs[: spaces - 1]
    table_x, table_y, table_f, out, left, right = refs[spaces - 1 :]
    planes = keep.shape[1]
    modes_x = keep.shape[2]
    modes_z = table_f.shape[0] // modes_x
    width_y = out.shape[5]
    me = lax.axis_index("space")
    for k in range(modes_z):
        part = pl.ds(k * modes_x, modes_x)
        left[part, :] = table_f[part, :] * carried[part, :]
        right[part, :] = table_f[part, :] * left[part, :]
    y_high, y_low = table_y[0], table_y[1]
    x_high, x_low = table_x[0], table_x[1]
    for node, source in ((0, left), (1, right)):
        for z in range(planes):
            value = keep[node, z]
            for other in received:
                value = value + other[node, z]
            for k in range(modes_z):
                weight = interp_z[me * planes + z, k]
                value = value + weight * source[pl.ds(k * modes_x, modes_x), :]
            high, low = split(value)
            wide = dot(high, y_high) + (dot(low, y_high) + dot(high, y_low))
            high, low = split(wide)
            fine = dot(x_high, high) + (dot(x_low, high) + dot(x_high, low))
            for s in range(2):
                out[0, node, s, z] = swept[node, s, z] + fine[:, s * width_y : (s + 1) * width_y]


def local(nodes, initial):
    count, spaces = lax.axis_size("tm"), lax.axis_size("space")
    planes, width_x, width_y = initial.shape[1:]
    modes_x, modes_y, modes_z = width_x // 2, width_y // 2, planes * spaces // 2
    half, lanes = planes // 2, 2 * modes_y
    devices = count * spaces
    f32 = jnp.float32
    shape = jax.ShapeDtypeStruct
    vmem, smem = pl.BlockSpec(memory_space=pltpu.VMEM), pl.BlockSpec(memory_space=pltpu.SMEM)
    params = pltpu.CompilerParams(vmem_limit_bytes=24 << 20)
    sides = 1 if spaces == 2 else 2

    forward_z = jnp.asarray(sine_table(modes_z, modes_z).T, f32)
    interp_z = jnp.asarray(sine_table(planes * spaces, modes_z), f32)
    forward_x = jnp.stack([jnp.asarray(t) for t in np_split(restricted(modes_x))])
    forward_y = jnp.stack([jnp.asarray(t) for t in np_split(doubled(restricted(modes_y).T))])
    interp_x = jnp.stack([jnp.asarray(t) for t in np_split(sine_table(width_x, modes_x))])
    interp_y = jnp.stack([jnp.asarray(t) for t in np_split(doubled(sine_table(width_y, modes_y).T))])
    factors = jnp.asarray(factor_table(modes_z, modes_x, modes_y))

    plane_pair = shape((2, 2, width_x, width_y), f32)
    prepared = pl.pallas_call(
        functools.partial(prepare_kernel, spaces, count),
        out_shape=[shape((2, planes, width_x, width_y), f32)] + [plane_pair] * (2 * sides),
        in_specs=[vmem, vmem],
        out_specs=[vmem] * (1 + 2 * sides),
        compiler_params=params,
        name="prepare",
    )(nodes, initial)
    finish = prepared[0]
    prior = lax.ppermute(finish, "tm", [(t, t + 1) for t in range(count - 1)])
    halos = []
    for n in range(sides):
        if spaces == 2:
            moves = [(0, 1), (1, 0)]
        else:
            step = -1 if n == 0 else 1
            moves = [(s, s + step) for s in range(spaces) if 0 <= s + step < spaces]
        across = [(t * spaces + a, (t + 1) % count * spaces + b) for t in range(count) for a, b in moves]
        own = lax.ppermute(prepared[1 + 2 * n], "space", moves)
        diagonal = lax.ppermute(prepared[2 + 2 * n], AXES, across)
        halos.append((own, diagonal))
    if spaces != 2:
        halos = halos[::-1]
    halo_args = [value for pair in halos for value in pair]

    rows = modes_z * modes_x
    block = shape((2, planes, modes_x, lanes), f32)
    fields = 3 * half + 2 * sides
    whole = pltpu.VMEM((2, planes, width_x, width_y), f32)
    results = pl.pallas_call(
        functools.partial(sweep_kernel, spaces),
        out_shape=[shape((2, 2, planes, width_x, width_y), f32), shape((rows, lanes), f32)] + [block] * spaces,
        in_specs=[smem, smem] + [vmem] * (3 + 2 * sides + 3),
        out_specs=[vmem] * (2 + spaces),
        scratch_shapes=[whole] * 5
        + [pltpu.VMEM((fields * width_x, 2 * width_y), f32), pltpu.VMEM((fields, modes_x, lanes), f32)],
        compiler_params=params,
        name="sweep",
    )(forward_z, interp_z, nodes, initial, prior, *halo_args, forward_x, forward_y, factors)
    swept, element, keep, sends = results[0], results[1], results[2], results[3:]

    share = rows // devices
    pieces = lax.all_to_all(element.reshape(devices, share, lanes), AXES, 0, 0, tiled=True)
    received = [
        lax.ppermute(send, "space", [(s, (s + j) % spaces) for s in range(spaces)])
        for j, send in enumerate(sends, 1)
    ]
    place = lax.axis_index(AXES) * share
    own_factor = lax.dynamic_slice_in_dim(factors, place, share, axis=0)
    carried = pl.pallas_call(
        functools.partial(chain_kernel, count, spaces),
        out_shape=shape((devices, share, lanes), f32),
        in_specs=[vmem, vmem],
        out_specs=vmem,
        compiler_params=params,
        name="chain",
    )(pieces, own_factor)
    carried = lax.all_to_all(carried, AXES, 0, 0, tiled=True).reshape(rows, lanes)

    return pl.pallas_call(
        functools.partial(finish_kernel, spaces),
        out_shape=shape((1, 2, 2, planes, width_x, width_y), f32),
        in_specs=[smem] + [vmem] * (3 + spaces - 1 + 3),
        out_specs=vmem,
        scratch_shapes=[pltpu.VMEM((rows, lanes), f32)] * 2,
        compiler_params=params,
        name="finish",
    )(interp_z, carried, swept, keep, *received, interp_x, interp_y, factors)


def solution(mesh):
    in_specs = (P("tm", None, None, "space", None, None), P(None, "space", None, None))
    out_specs = P("tm", None, None, "space", None, None)
    return jax.shard_map(local, mesh=mesh, in_specs=in_specs, out_specs=out_specs, check_vma=False)
```

```python
import functools
import math

import jax
import jax.numpy as jnp
import numpy as np
from jax import lax
from jax.experimental import pallas as pl
from jax.experimental.pallas import tpu as pltpu
from jax.sharding import PartitionSpec as P

diffusion = (0.5, 0.25)
feed_rate = 0.04
kill_rate = 0.06
decay = (feed_rate, feed_rate + kill_rate)
slice_length = 0.5
node_step = 0.25
sweep_weights = ((5.0 / 24.0, 1.0 / 3.0, -1.0 / 24.0), (-1.0 / 24.0, 1.0 / 3.0, 5.0 / 24.0))
(T00, T01, T02), (T10, T11, T12) = [[slice_length * w for w in row] for row in sweep_weights]
AXES = ("tm", "space")
RIM = 8
TABLES = 6


def sine_table(points, modes):
    place = np.arange(points) + 0.5
    order = np.arange(modes) + 1.0
    weight = np.where(np.arange(modes) == modes - 1, math.sqrt(0.5), 1.0)
    return math.sqrt(2.0 / modes) * weight[None, :] * np.sin(math.pi / points * place[:, None] * order[None, :])


def np_split(table):
    table = np.asarray(table, np.float32)
    high = table.astype(jnp.bfloat16)
    low = (table - high.astype(np.float32)).astype(jnp.bfloat16)
    return high, low


def restricted(modes):
    return np.repeat(sine_table(modes, modes).T, 2, axis=1) * 0.5


def doubled(table):
    rows, columns = table.shape
    both = np.zeros((2 * rows, 2 * columns))
    both[:rows, :columns] = table
    both[rows:, columns:] = table
    return both


def eigen(count):
    return 2.0 * np.cos(math.pi * (np.arange(count) + 1.0) / count) - 2.0


def factor_table(modes_z, modes_x, modes_y):
    total = (eigen(modes_z)[:, None, None] + eigen(modes_x)[None, :, None] + eigen(modes_y)[None, None, :]) / 4.0
    linear = np.stack([diffusion[i] * total - decay[i] for i in range(2)], axis=2)
    factor = 1.0 / (1.0 - node_step * linear)
    return np.asarray(factor.reshape(modes_z * modes_x, 2 * modes_y), np.float32)


def split(table):
    high = table.astype(jnp.bfloat16)
    low = (table - high.astype(jnp.float32)).astype(jnp.bfloat16)
    return high, low


def dot(a, b):
    return jnp.dot(a, b, preferred_element_type=jnp.float32)


def pick(values, index):
    result = jnp.float32(values[0])
    for n, value in enumerate(values[1:], 1):
        result = jnp.where(index == n, jnp.float32(value), result)
    return result


def rates(p, q, near_p, near_q):
    reaction = (1.0 + p) * q * q
    return (
        diffusion[0] * near_p - (6.0 * diffusion[0] + decay[0]) * p - reaction,
        diffusion[1] * near_q - (6.0 * diffusion[1] + decay[1]) * q + reaction,
    )


def plane(ref, s, z):
    return ref[s, z, pl.ds(RIM, ref.shape[2] - 2 * RIM), :]


def in_plane(ref, s, z):
    rows, lanes = ref.shape[2] - 2 * RIM, ref.shape[3]
    v = plane(ref, s, z)
    lane = lax.broadcasted_iota(jnp.int32, (rows, lanes), 1)
    left = jnp.where(lane == lanes - 1, 0.0, pltpu.roll(v, lanes - 1, 1))
    right = jnp.where(lane == 0, 0.0, pltpu.roll(v, 1, 1))
    rims = ref[s, z, pl.ds(RIM - 1, rows), :] + ref[s, z, pl.ds(RIM + 1, rows), :]
    return rims + (left + right)


def rates_at(ref, z, around=None):
    planes = ref.shape[1]
    if around is None:
        around = [n for n in (z - 1, z + 1) if 0 <= n < planes]
    near = [sum((plane(ref, s, n) for n in around), in_plane(ref, s, z)) for s in range(2)]
    return rates(plane(ref, 0, z), plane(ref, 1, z), *near)


def set_plane(ref, s, z, value):
    ref[s, z, pl.ds(RIM, ref.shape[2] - 2 * RIM), :] = value


def clear_rims(ref):
    rows = ref.shape[2]
    zero = jnp.zeros((RIM, ref.shape[3]), jnp.float32)
    for s in range(2):
        for z in range(ref.shape[1]):
            ref[s, z, pl.ds(0, RIM), :] = zero
            ref[s, z, pl.ds(rows - RIM, RIM), :] = zero


def facing(spaces):
    if spaces == 2:
        return [1 - lax.axis_index("space")]
    return [0, 1]


def edge_plane(side, planes):
    return side * (planes - 1)


def edge_pair(side, planes):
    return side * (planes - 2)


def load_kernel(spaces, nodes, out, sem):
    planes = nodes.shape[3]
    place = edge_pair(facing(spaces)[0], planes) if spaces == 2 else 0
    copy = pltpu.make_async_copy(nodes.at[0, 1, :, pl.ds(place, out.shape[1])], out, sem.at[0])
    copy.start()
    copy.wait()


def early_kernel(spaces, nodes, *refs):
    sides = facing(spaces)
    tables, refs = refs[:TABLES], refs[TABLES:]
    one, rest, refs = refs[0], refs[1], refs[2:]
    outs, near, refs = refs[: len(sides)], refs[len(sides) : len(sides) + TABLES], refs[len(sides) + TABLES :]
    inner, (middle, finish, sems) = refs[:-3], refs[-3:]
    planes, rows = nodes.shape[3], nodes.shape[4]
    copies = [
        pltpu.make_async_copy(nodes.at[0, n], target.at[:, :, pl.ds(RIM, rows), :], sems.at[n])
        for n, target in enumerate((middle, finish))
    ]
    device = lax.axis_index("tm") * spaces + lax.axis_index("space")
    sources = [tables[0].at[device], *tables[1:]]
    others = [pltpu.make_async_copy(a, b, sems.at[2 + n]) for n, (a, b) in enumerate(zip(sources, near))]
    if inner:
        cut = pl.ds(2 - 2 * sides[0], planes - 2)
        others.append(pltpu.make_async_copy(nodes.at[0, 1, :, cut], inner[0], sems.at[2 + TABLES]))
    for copy in copies + others:
        copy.start()
    clear_rims(middle)
    clear_rims(finish)
    for copy in copies:
        copy.wait()
    for z in range(planes):
        f1, f2 = rates_at(middle, z), rates_at(finish, z)
        for s in range(2):
            one[s, z] = T01 * f1[s] + T02 * f2[s]
            rest[s, z] = (T11 - node_step) * f1[s] + T12 * f2[s]
    for side, out in zip(sides, outs):
        edge = edge_plane(side, planes)
        for s in range(2):
            mid, end = plane(middle, s, edge), plane(finish, s, edge)
            out[0, s] = T01 * mid + T02 * end
            out[1, s] = node_step * one[s, edge] + (T11 - node_step) * mid + T12 * end
    for copy in others:
        copy.wait()


def merge_kernel(spaces, initial, edge, *refs):
    count = 1 if spaces == 2 else 2
    owns, outs, (held, sem) = refs[:count], refs[count : 2 * count], refs[2 * count :]
    planes, rows = initial.shape[1], initial.shape[2]
    is_first = lax.axis_index("tm") == 0
    sides = facing(spaces)
    shift = edge_pair(sides[0], planes) if spaces == 2 else 0

    @pl.when(is_first)
    def _():
        copy = pltpu.make_async_copy(
            initial.at[:, pl.ds(shift, edge.shape[1])], held.at[:, :, pl.ds(RIM, rows), :], sem.at[0]
        )
        copy.start()
        copy.wait()

    @pl.when(jnp.logical_not(is_first))
    def _():
        for s in range(2):
            for z in range(edge.shape[1]):
                set_plane(held, s, z, edge[s, z])

    clear_rims(held)
    for side, own, out in zip(sides, owns, outs):
        first = edge_plane(side, planes) - shift
        second = first + 1 - 2 * side
        slope = rates_at(held, first, [second])
        for s in range(2):
            start = plane(held, s, first)
            out[0, s] = own[0, s] + T00 * start
            out[1, s] = own[1, s] + (node_step + T10) * start + (node_step * T00) * slope[s]


def start_kernel(spaces, initial, *refs):
    parts, refs = refs[: 2 if spaces == 2 else 1], refs[2 if spaces == 2 else 1 :]
    one_in, rest_in, start, one, rest, x_base, y_base, sem = refs
    planes, rows = initial.shape[1], initial.shape[2]
    is_first = lax.axis_index("tm") == 0

    @pl.when(is_first)
    def _():
        copy = pltpu.make_async_copy(initial, start.at[:, :, pl.ds(RIM, rows), :], sem.at[0])
        copy.start()
        copy.wait()

    @pl.when(jnp.logical_not(is_first))
    def _():
        if spaces == 2:
            side = facing(spaces)[0]
            places = [edge_pair(side, planes), 2 - 2 * side]
        else:
            places = [0]
        for place, part in zip(places, parts):
            for z in range(part.shape[1]):
                for s in range(2):
                    set_plane(start, s, place + z, part[s, z])

    clear_rims(start)
    for c in range(planes // 2):
        total = [0.0, 0.0]
        for z in (2 * c, 2 * c + 1):
            f0 = rates_at(start, z)
            for s in range(2):
                one[s, z] = plane(start, s, z) + T00 * f0[s] + one_in[s, z]
                rest[s, z] = T10 * f0[s] + rest_in[s, z]
                total[s] = total[s] + f0[s]
        for s in range(2):
            both = plane(start, s, 2 * c) + plane(start, s, 2 * c + 1)
            x_base[s, c] = (0.5 * T00) * total[s] + jnp.where(is_first, 0.5 * both, 0.0)
            y_base[s, c] = (0.5 * T10) * total[s]


def sweep_kernel(spaces, start, early, rest, x_base, y_base, *refs):
    sides = facing(spaces)
    count = len(sides)
    halos, owns, refs = refs[:count], refs[count : 2 * count], refs[2 * count :]
    table_x, table_y, table_f, one, two, element = refs[:6]
    targets, (slope1, stack, along, spec, x_part, y_part) = refs[6 : 6 + spaces], refs[6 + spaces :]
    planes = early.shape[1]
    half = planes // 2
    modes_x = table_x.shape[1]
    modes_z = table_f.shape[0] // modes_x
    rows, width_y = early.shape[2], early.shape[3]
    lanes = table_f.shape[1]
    me = lax.axis_index("space")
    clear_rims(one)
    clear_rims(two)
    for z in range(planes):
        for s in range(2):
            set_plane(one, s, z, early[s, z])
    for side, halo, own in zip(sides, halos, owns):
        edge = edge_plane(side, planes)
        for s in range(2):
            d = diffusion[s]
            set_plane(one, s, edge, plane(one, s, edge) + d * halo[0, s])
            back = T00 * plane(start, s, edge) + own[0, s]
            if spaces != 2:
                back = jnp.where(me == (0 if side == 0 else spaces - 1), 0.0, back)
            rest[s, edge] = rest[s, edge] + d * (halo[1, s] + (node_step * d) * back)
    for z in range(planes):
        g1 = rates_at(one, z)
        for s in range(2):
            first = plane(one, s, z)
            second = first + node_step * g1[s] + rest[s, z]
            set_plane(two, s, z, second)
            slope1[s, z // 2] = g1[s] if z % 2 == 0 else slope1[s, z // 2] + g1[s]

    def put(slot, s, value):
        stack[pl.ds(slot * rows, rows), pl.ds(s * width_y, width_y)] = value

    for n, side in enumerate(sides):
        edge = edge_plane(side, planes)
        for s in range(2):
            d = 0.5 * diffusion[s]
            zero, first, second = plane(start, s, edge), plane(one, s, edge), plane(two, s, edge)
            put(3 * half + 2 * n, s, d * (T00 * zero + T01 * first + T02 * second))
            put(3 * half + 2 * n + 1, s, d * (T10 * zero + T11 * first + T12 * second))
    for c in range(half):
        pair = [rates_at(two, 2 * c), rates_at(two, 2 * c + 1)]
        for s in range(2):
            g1, g2 = slope1[s, c], pair[0][s] + pair[1][s]
            first = 0.5 * (plane(one, s, 2 * c) + plane(one, s, 2 * c + 1))
            second = 0.5 * (plane(two, s, 2 * c) + plane(two, s, 2 * c + 1))
            put(c, s, x_base[s, c] + (0.5 * T01) * g1 + (0.5 * T02) * g2 - first)
            put(half + c, s, y_base[s, c] + (0.5 * T11) * g1 + (0.5 * T12) * g2 + (first - second))
            put(2 * half + c, s, second)
    fields = 3 * half + 2 * count
    for f in range(fields):
        high, low = split(stack[pl.ds(f * rows, rows), :])
        both = dot(high, table_y[...])
        along[:, pl.ds(f * lanes, lanes)] = both[:, :lanes] + (both[:, lanes:] + dot(low, table_y[:, :lanes]))
    for f in range(0, fields, 2):
        part = pl.ds(f * lanes, 2 * lanes)
        high, low = split(along[:, part])
        both = dot(table_x[...].reshape(2 * modes_x, rows), high)
        spec[:, part] = both[:modes_x] + (both[modes_x:] + dot(table_x[0], low))

    def at(f):
        return spec[:, pl.ds(f * lanes, lanes)]

    weights_z = sine_table(modes_z, modes_z)
    for k in range(modes_z):
        part = pl.ds(k * modes_x, modes_x)
        factor = table_f[part, :]
        weights = [pick([weights_z[d * half + c, k] for d in range(spaces)], me) for c in range(half)]
        x = sum(weights[c] * at(c) for c in range(half))
        y = sum(weights[c] * at(half + c) for c in range(half))
        e = sum(weights[c] * at(2 * half + c) for c in range(half))
        for n, side in enumerate(sides):
            below = [weights_z[d * half - 1, k] if d else 0.0 for d in range(spaces)]
            above = [weights_z[(d + 1) * half, k] if d < spaces - 1 else 0.0 for d in range(spaces)]
            weight = pick([b if d else a for d, (a, b) in enumerate(zip(above, below))] if spaces == 2 else (below, above)[side], me)
            x = x + weight * at(3 * half + 2 * n)
            y = y + weight * at(3 * half + 2 * n + 1)
        x = factor * x
        y = factor * (x + y)
        x_part[part, :] = x
        y_part[part, :] = y
        element[part, :] = y + e
    table = sine_table(planes * spaces, modes_z)
    for j, target in enumerate(targets):
        device = lax.rem(me + j, spaces)
        for z in range(planes):
            weights = [pick([table[d * planes + z, k] for d in range(spaces)], device) for k in range(modes_z)]
            for node, source in enumerate((x_part, y_part)):
                target[node, z] = sum(w * source[pl.ds(k * modes_x, modes_x), :] for k, w in enumerate(weights))


def chain_kernel(count, spaces, pieces, factor, *refs):
    out = refs[-1]
    gain = factor[...] * factor[...]
    state = jnp.zeros_like(gain)
    for t in range(count):
        for s in range(spaces):
            out[t * spaces + s] = state
        if t < count - 1:
            total = pieces[t * spaces]
            for s in range(1, spaces):
                total = total + pieces[t * spaces + s]
            state = gain * state + total


def finish_kernel(spaces, carried, one, two, keep, *refs):
    received = refs[: spaces - 1]
    table_x, table_y, table_f, out, left, right, wide, result, sems = refs[spaces - 1 :]
    planes, modes_x, lanes = keep.shape[1:]
    modes_z = table_f.shape[0] // modes_x
    width_y = out.shape[5]
    me = lax.axis_index("space")
    table = sine_table(planes * spaces, modes_z)
    for k in range(modes_z):
        part = pl.ds(k * modes_x, modes_x)
        left[part, :] = table_f[part, :] * carried[part, :]
        right[part, :] = table_f[part, :] * left[part, :]
    copies = []
    for node, source in ((0, left), (1, right)):
        for z in range(planes):
            value = keep[node, z]
            for other in received:
                value = value + other[node, z]
            for k in range(modes_z):
                weight = pick([table[d * planes + z, k] for d in range(spaces)], me)
                value = value + weight * source[pl.ds(k * modes_x, modes_x), :]
            high, low = split(value)
            wide[node * planes + z] = dot(jnp.concatenate([high, low], axis=1), table_y[0]) + dot(
                high, table_y[1, :lanes]
            )
    for node, swept in ((0, one), (1, two)):
        for z in range(planes):
            high, low = split(wide[node * planes + z])
            fine = dot(table_x[...], jnp.concatenate([high, high, low], axis=0))
            for s in range(2):
                result[node, s, z] = plane(swept, s, z) + fine[:, s * width_y : (s + 1) * width_y]
            copy = pltpu.make_async_copy(result.at[node, :, z], out.at[0, node, :, z], sems.at[node * planes + z])
            copy.start()
            copies.append(copy)
    for copy in copies:
        copy.wait()


def iteration(nodes, initial):
    count, spaces = lax.axis_size("tm"), lax.axis_size("space")
    planes, width_x, width_y = initial.shape[1:]
    modes_x, modes_y, modes_z = width_x // 2, width_y // 2, planes * spaces // 2
    half, lanes = planes // 2, 2 * modes_y
    devices = count * spaces
    f32 = jnp.float32
    shape = jax.ShapeDtypeStruct
    vmem, far = pl.BlockSpec(memory_space=pltpu.VMEM), pl.BlockSpec(memory_space=pltpu.HBM)
    params = pltpu.CompilerParams(vmem_limit_bytes=24 << 20)
    sides = 1 if spaces == 2 else 2
    sem = pltpu.SemaphoreType.DMA

    def in_hbm(value):
        return pltpu.with_memory_space_constraint(jnp.asarray(value), pltpu.HBM)

    nodes, initial = in_hbm(nodes), in_hbm(initial)
    rows = modes_z * modes_x
    share = rows // devices
    factors = factor_table(modes_z, modes_x, modes_y)
    high_x, low_x = np_split(sine_table(width_x, modes_x))
    high_y, low_y = np_split(doubled(sine_table(width_y, modes_y).T))
    tables = [
        factors.reshape(devices, share, lanes),
        np.stack(np_split(restricted(modes_x))),
        np.concatenate(np_split(doubled(restricted(modes_y).T)), axis=1),
        factors,
        np.concatenate([high_x, low_x, high_x], axis=1),
        np.stack([np.concatenate([high_y, high_y]), np.concatenate([low_y, low_y])]),
    ]
    near = [shape((share, lanes), f32)] + [shape(table.shape, table.dtype) for table in tables[1:]]

    plane_pair = shape((2, 2, width_x, width_y), f32)
    whole = shape((2, planes, width_x, width_y), f32)
    rimmed = shape((2, planes, width_x + 2 * RIM, width_y), f32)
    cuts = [2, planes - 2] if spaces == 2 else [planes]
    edge = pl.pallas_call(
        functools.partial(load_kernel, spaces),
        out_shape=shape((2, cuts[0], width_x, width_y), f32),
        in_specs=[far],
        out_specs=vmem,
        scratch_shapes=[sem((1,))],
        compiler_params=params,
        name="load",
    )(nodes)
    onward = [(t, t + 1) for t in range(count - 1)]
    parts = [lax.ppermute(edge, "tm", onward)]
    one, rest, *others = pl.pallas_call(
        functools.partial(early_kernel, spaces),
        out_shape=[whole] * 2
        + [plane_pair] * sides
        + near
        + [shape((2, cut, width_x, width_y), f32) for cut in cuts[1:]],
        in_specs=[far] * (1 + TABLES),
        out_specs=[vmem] * (2 + sides + TABLES + len(cuts) - 1),
        scratch_shapes=[pltpu.VMEM(rimmed.shape, f32)] * 2 + [sem((3 + TABLES,))],
        compiler_params=params,
        name="early",
    )(nodes, *[in_hbm(table) for table in tables])
    owns, near, inner = others[:sides], others[sides : sides + TABLES], others[sides + TABLES :]
    parts += [lax.ppermute(part, "tm", onward) for part in inner]
    merged = pl.pallas_call(
        functools.partial(merge_kernel, spaces),
        out_shape=[plane_pair] * sides,
        in_specs=[far] + [vmem] * (1 + sides),
        out_specs=[vmem] * sides,
        scratch_shapes=[pltpu.VMEM((2, cuts[0], width_x + 2 * RIM, width_y), f32), sem((1,))],
        compiler_params=params,
        name="merge",
    )(initial, parts[0], *owns)
    halos = []
    for n, part in enumerate(merged):
        if spaces == 2:
            moves = [(0, 1), (1, 0)]
        else:
            step = -1 if n == 0 else 1
            moves = [(s, s + step) for s in range(spaces) if 0 <= s + step < spaces]
        halos.append(lax.ppermute(part, "space", moves))
    if spaces != 2:
        halos = halos[::-1]
    start, one, rest, *bases = pl.pallas_call(
        functools.partial(start_kernel, spaces),
        out_shape=[rimmed] + [whole] * 2 + [shape((2, half, width_x, width_y), f32)] * 2,
        in_specs=[far] + [vmem] * (len(cuts) + 2),
        out_specs=[vmem] * 5,
        scratch_shapes=[sem((1,))],
        compiler_params=params,
        name="begin",
    )(initial, *parts, one, rest)

    block = shape((2, planes, modes_x, lanes), f32)
    fields = 3 * half + 2 * sides
    one, two, element, keep, *sends = pl.pallas_call(
        functools.partial(sweep_kernel, spaces),
        out_shape=[rimmed] * 2 + [shape((rows, lanes), f32)] + [block] * spaces,
        in_specs=[vmem] * (5 + 2 * sides + 3),
        out_specs=[vmem] * (3 + spaces),
        scratch_shapes=[
            pltpu.VMEM((2, half, width_x, width_y), f32),
            pltpu.VMEM((fields * width_x, 2 * width_y), f32),
            pltpu.VMEM((width_x, fields * lanes), f32),
            pltpu.VMEM((modes_x, fields * lanes), f32),
            pltpu.VMEM((rows, lanes), f32),
            pltpu.VMEM((rows, lanes), f32),
        ],
        compiler_params=params,
        name="sweep",
    )(start, one, rest, *bases, *halos, *owns, *near[1:4])

    received = []
    for j, send in enumerate(sends, 1):
        received.append(lax.ppermute(send, "space", [(s, (s + j) % spaces) for s in range(spaces)]))
    pieces = lax.all_to_all(element.reshape(devices, share, lanes), AXES, 0, 0, tiled=True)
    carried = pl.pallas_call(
        functools.partial(chain_kernel, count, spaces),
        out_shape=shape((devices, share, lanes), f32),
        in_specs=[vmem, vmem] + [pl.BlockSpec(memory_space=pl.ANY)] * (spaces - 1),
        out_specs=vmem,
        compiler_params=params,
        name="chain",
    )(pieces, near[0], *received)
    carried = lax.all_to_all(carried, AXES, 0, 0, tiled=True).reshape(rows, lanes)

    return pl.pallas_call(
        functools.partial(finish_kernel, spaces),
        out_shape=shape((1, 2, 2, planes, width_x, width_y), f32),
        in_specs=[vmem] * (4 + spaces - 1 + 3),
        out_specs=far,
        scratch_shapes=[pltpu.VMEM((rows, lanes), f32)] * 2
        + [
            pltpu.VMEM((2 * planes, modes_x, 2 * width_y), f32),
            pltpu.VMEM((2, 2, planes, width_x, width_y), f32),
            sem((2 * planes,)),
        ],
        compiler_params=params,
        name="finish",
    )(carried, one, two, keep, *received, near[4], near[5], near[3])


def solution(mesh):
    in_specs = (P("tm", None, None, "space", None, None), P(None, "space", None, None))
    out_specs = P("tm", None, None, "space", None, None)
    return jax.shard_map(iteration, mesh=mesh, in_specs=in_specs, out_specs=out_specs, check_vma=False)
```

```python
import functools
import math

import jax
import jax.numpy as jnp
import numpy as np
from jax import lax
from jax.experimental import pallas as pl
from jax.experimental.pallas import tpu as pltpu
from jax.sharding import PartitionSpec as P

diffusion = (0.5, 0.25)
feed_rate = 0.04
kill_rate = 0.06
decay = (feed_rate, feed_rate + kill_rate)
slice_length = 0.5
node_step = 0.25
sweep_weights = ((5.0 / 24.0, 1.0 / 3.0, -1.0 / 24.0), (-1.0 / 24.0, 1.0 / 3.0, 5.0 / 24.0))
(T00, T01, T02), (T10, T11, T12) = [[slice_length * w for w in row] for row in sweep_weights]
AXES = ("tm", "space")
RIM = 8
TABLES = 6


def sine_table(points, modes):
    place = np.arange(points) + 0.5
    order = np.arange(modes) + 1.0
    weight = np.where(np.arange(modes) == modes - 1, math.sqrt(0.5), 1.0)
    return math.sqrt(2.0 / modes) * weight[None, :] * np.sin(math.pi / points * place[:, None] * order[None, :])


def np_split(table):
    table = np.asarray(table, np.float32)
    high = table.astype(jnp.bfloat16)
    low = (table - high.astype(np.float32)).astype(jnp.bfloat16)
    return high, low


def restricted(modes):
    return np.repeat(sine_table(modes, modes).T, 2, axis=1) * 0.5


def doubled(table):
    rows, columns = table.shape
    both = np.zeros((2 * rows, 2 * columns))
    both[:rows, :columns] = table
    both[rows:, columns:] = table
    return both


def eigen(count):
    return 2.0 * np.cos(math.pi * (np.arange(count) + 1.0) / count) - 2.0


def factor_table(modes_z, modes_x, modes_y):
    total = (eigen(modes_z)[:, None, None] + eigen(modes_x)[None, :, None] + eigen(modes_y)[None, None, :]) / 4.0
    linear = np.stack([diffusion[i] * total - decay[i] for i in range(2)], axis=2)
    factor = 1.0 / (1.0 - node_step * linear)
    return np.asarray(factor.reshape(modes_z * modes_x, 2 * modes_y), np.float32)


def split(table):
    high = table.astype(jnp.bfloat16)
    low = (table - high.astype(jnp.float32)).astype(jnp.bfloat16)
    return high, low


def dot(a, b):
    return jnp.dot(a, b, preferred_element_type=jnp.float32)


def pick(values, index):
    result = jnp.float32(values[0])
    for n, value in enumerate(values[1:], 1):
        result = jnp.where(index == n, jnp.float32(value), result)
    return result


def rates(p, q, near_p, near_q):
    reaction = (1.0 + p) * q * q
    return (
        diffusion[0] * near_p - (6.0 * diffusion[0] + decay[0]) * p - reaction,
        diffusion[1] * near_q - (6.0 * diffusion[1] + decay[1]) * q + reaction,
    )


def plane(ref, s, z):
    return ref[s, z, pl.ds(RIM, ref.shape[2] - 2 * RIM), :]


def in_plane(ref, s, z):
    rows, lanes = ref.shape[2] - 2 * RIM, ref.shape[3]
    v = plane(ref, s, z)
    lane = lax.broadcasted_iota(jnp.int32, (rows, lanes), 1)
    left = jnp.where(lane == lanes - 1, 0.0, pltpu.roll(v, lanes - 1, 1))
    right = jnp.where(lane == 0, 0.0, pltpu.roll(v, 1, 1))
    rims = ref[s, z, pl.ds(RIM - 1, rows), :] + ref[s, z, pl.ds(RIM + 1, rows), :]
    return rims + (left + right)


def rates_at(ref, z, around=None):
    planes = ref.shape[1]
    if around is None:
        around = [n for n in (z - 1, z + 1) if 0 <= n < planes]
    near = [sum((plane(ref, s, n) for n in around), in_plane(ref, s, z)) for s in range(2)]
    return rates(plane(ref, 0, z), plane(ref, 1, z), *near)


def set_plane(ref, s, z, value):
    ref[s, z, pl.ds(RIM, ref.shape[2] - 2 * RIM), :] = value


def clear_rims(ref):
    rows = ref.shape[2]
    zero = jnp.zeros((RIM, ref.shape[3]), jnp.float32)
    for s in range(2):
        for z in range(ref.shape[1]):
            ref[s, z, pl.ds(0, RIM), :] = zero
            ref[s, z, pl.ds(rows - RIM, RIM), :] = zero


def facing(spaces):
    if spaces == 2:
        return [1 - lax.axis_index("space")]
    return [0, 1]


def edge_plane(side, planes):
    return side * (planes - 1)


def edge_pair(side, planes):
    return side * (planes - 2)


def send_from(count, nodes, initial, cut, target, sem):
    is_last = lax.axis_index("tm") == count - 1

    def copy(source):
        return pltpu.make_async_copy(source.at[:, cut], target, sem)

    @pl.when(is_last)
    def _():
        copy(initial).start()

    @pl.when(jnp.logical_not(is_last))
    def _():
        copy(nodes.at[0, 1]).start()

    return copy(initial)


def load_kernel(spaces, count, nodes, initial, out, sem):
    planes = nodes.shape[3]
    place = edge_pair(facing(spaces)[0], planes) if spaces == 2 else 0
    send_from(count, nodes, initial, pl.ds(place, out.shape[1]), out, sem.at[0]).wait()


def early_kernel(spaces, count, nodes, initial, *refs):
    sides = facing(spaces)
    tables, refs = refs[:TABLES], refs[TABLES:]
    one, rest, refs = refs[0], refs[1], refs[2:]
    outs, near, refs = refs[: len(sides)], refs[len(sides) : len(sides) + TABLES], refs[len(sides) + TABLES :]
    inner, (middle, finish, sems) = refs[:-3], refs[-3:]
    planes, rows = nodes.shape[3], nodes.shape[4]
    copies = [
        pltpu.make_async_copy(nodes.at[0, n], target.at[:, :, pl.ds(RIM, rows), :], sems.at[n])
        for n, target in enumerate((middle, finish))
    ]
    device = lax.axis_index("tm") * spaces + lax.axis_index("space")
    sources = [tables[0].at[device], *tables[1:]]
    others = [pltpu.make_async_copy(a, b, sems.at[2 + n]) for n, (a, b) in enumerate(zip(sources, near))]
    for copy in copies + others:
        copy.start()
    if inner:
        cut = pl.ds(2 - 2 * sides[0], planes - 2)
        others.append(send_from(count, nodes, initial, cut, inner[0], sems.at[2 + TABLES]))
    clear_rims(middle)
    clear_rims(finish)
    for copy in copies:
        copy.wait()
    for z in range(planes):
        f1, f2 = rates_at(middle, z), rates_at(finish, z)
        for s in range(2):
            one[s, z] = T01 * f1[s] + T02 * f2[s]
            rest[s, z] = (T11 - node_step) * f1[s] + T12 * f2[s]
    for side, out in zip(sides, outs):
        edge = edge_plane(side, planes)
        for s in range(2):
            mid, end = plane(middle, s, edge), plane(finish, s, edge)
            out[0, s] = T01 * mid + T02 * end
            out[1, s] = node_step * one[s, edge] + (T11 - node_step) * mid + T12 * end
    for copy in others:
        copy.wait()


def merge_kernel(spaces, planes, edge, *refs):
    count = 1 if spaces == 2 else 2
    owns, outs, held = refs[:count], refs[count : 2 * count], refs[2 * count]
    sides = facing(spaces)
    shift = edge_pair(sides[0], planes) if spaces == 2 else 0
    for s in range(2):
        for z in range(edge.shape[1]):
            set_plane(held, s, z, edge[s, z])
    clear_rims(held)
    for side, own, out in zip(sides, owns, outs):
        first = edge_plane(side, planes) - shift
        second = first + 1 - 2 * side
        slope = rates_at(held, first, [second])
        for s in range(2):
            start = plane(held, s, first)
            out[0, s] = own[0, s] + T00 * start
            out[1, s] = own[1, s] + (node_step + T10) * start + (node_step * T00) * slope[s]


def start_kernel(spaces, *refs):
    parts, refs = refs[: 2 if spaces == 2 else 1], refs[2 if spaces == 2 else 1 :]
    one_in, rest_in, start, one, rest, x_base, y_base = refs
    planes = one.shape[1]
    is_first = lax.axis_index("tm") == 0
    if spaces == 2:
        side = facing(spaces)[0]
        places = [edge_pair(side, planes), 2 - 2 * side]
    else:
        places = [0]
    for place, part in zip(places, parts):
        for z in range(part.shape[1]):
            for s in range(2):
                set_plane(start, s, place + z, part[s, z])
    clear_rims(start)
    for c in range(planes // 2):
        total = [0.0, 0.0]
        for z in (2 * c, 2 * c + 1):
            f0 = rates_at(start, z)
            for s in range(2):
                one[s, z] = plane(start, s, z) + T00 * f0[s] + one_in[s, z]
                rest[s, z] = T10 * f0[s] + rest_in[s, z]
                total[s] = total[s] + f0[s]
        for s in range(2):
            both = plane(start, s, 2 * c) + plane(start, s, 2 * c + 1)
            x_base[s, c] = (0.5 * T00) * total[s] + jnp.where(is_first, 0.5 * both, 0.0)
            y_base[s, c] = (0.5 * T10) * total[s]


def sweep_kernel(spaces, start, early, rest, x_base, y_base, *refs):
    sides = facing(spaces)
    count = len(sides)
    halos, owns, refs = refs[:count], refs[count : 2 * count], refs[2 * count :]
    table_x, table_y, table_f, one, two, element = refs[:6]
    targets, (slope1, stack, along, spec, x_part, y_part) = refs[6 : 6 + spaces], refs[6 + spaces :]
    planes = early.shape[1]
    half = planes // 2
    modes_x = table_x.shape[1]
    modes_z = table_f.shape[0] // modes_x
    rows, width_y = early.shape[2], early.shape[3]
    lanes = table_f.shape[1]
    me = lax.axis_index("space")
    clear_rims(one)
    clear_rims(two)
    for z in range(planes):
        for s in range(2):
            set_plane(one, s, z, early[s, z])
    for side, halo, own in zip(sides, halos, owns):
        edge = edge_plane(side, planes)
        for s in range(2):
            d = diffusion[s]
            set_plane(one, s, edge, plane(one, s, edge) + d * halo[0, s])
            back = T00 * plane(start, s, edge) + own[0, s]
            if spaces != 2:
                back = jnp.where(me == (0 if side == 0 else spaces - 1), 0.0, back)
            rest[s, edge] = rest[s, edge] + d * (halo[1, s] + (node_step * d) * back)
    for z in range(planes):
        g1 = rates_at(one, z)
        for s in range(2):
            first = plane(one, s, z)
            second = first + node_step * g1[s] + rest[s, z]
            set_plane(two, s, z, second)
            slope1[s, z // 2] = g1[s] if z % 2 == 0 else slope1[s, z // 2] + g1[s]

    def put(slot, s, value):
        stack[pl.ds(slot * rows, rows), pl.ds(s * width_y, width_y)] = value

    for n, side in enumerate(sides):
        edge = edge_plane(side, planes)
        for s in range(2):
            d = 0.5 * diffusion[s]
            zero, first, second = plane(start, s, edge), plane(one, s, edge), plane(two, s, edge)
            put(3 * half + 2 * n, s, d * (T00 * zero + T01 * first + T02 * second))
            put(3 * half + 2 * n + 1, s, d * (T10 * zero + T11 * first + T12 * second))
    for c in range(half):
        pair = [rates_at(two, 2 * c), rates_at(two, 2 * c + 1)]
        for s in range(2):
            g1, g2 = slope1[s, c], pair[0][s] + pair[1][s]
            first = 0.5 * (plane(one, s, 2 * c) + plane(one, s, 2 * c + 1))
            second = 0.5 * (plane(two, s, 2 * c) + plane(two, s, 2 * c + 1))
            put(c, s, x_base[s, c] + (0.5 * T01) * g1 + (0.5 * T02) * g2 - first)
            put(half + c, s, y_base[s, c] + (0.5 * T11) * g1 + (0.5 * T12) * g2 + (first - second))
            put(2 * half + c, s, second)
    fields = 3 * half + 2 * count
    for f in range(fields):
        high, low = split(stack[pl.ds(f * rows, rows), :])
        both = dot(high, table_y[...])
        along[:, pl.ds(f * lanes, lanes)] = both[:, :lanes] + (both[:, lanes:] + dot(low, table_y[:, :lanes]))
    for f in range(0, fields, 2):
        part = pl.ds(f * lanes, 2 * lanes)
        high, low = split(along[:, part])
        both = dot(table_x[...].reshape(2 * modes_x, rows), high)
        spec[:, part] = both[:modes_x] + (both[modes_x:] + dot(table_x[0], low))

    def at(f):
        return spec[:, pl.ds(f * lanes, lanes)]

    weights_z = sine_table(modes_z, modes_z)
    for k in range(modes_z):
        part = pl.ds(k * modes_x, modes_x)
        factor = table_f[part, :]
        weights = [pick([weights_z[d * half + c, k] for d in range(spaces)], me) for c in range(half)]
        x = sum(weights[c] * at(c) for c in range(half))
        y = sum(weights[c] * at(half + c) for c in range(half))
        e = sum(weights[c] * at(2 * half + c) for c in range(half))
        for n, side in enumerate(sides):
            below = [weights_z[d * half - 1, k] if d else 0.0 for d in range(spaces)]
            above = [weights_z[(d + 1) * half, k] if d < spaces - 1 else 0.0 for d in range(spaces)]
            weight = pick([b if d else a for d, (a, b) in enumerate(zip(above, below))] if spaces == 2 else (below, above)[side], me)
            x = x + weight * at(3 * half + 2 * n)
            y = y + weight * at(3 * half + 2 * n + 1)
        x = factor * x
        y = factor * (x + y)
        x_part[part, :] = x
        y_part[part, :] = y
        element[part, :] = y + e
    table = sine_table(planes * spaces, modes_z)
    for j, target in enumerate(targets):
        device = lax.rem(me + j, spaces)
        for z in range(planes):
            weights = [pick([table[d * planes + z, k] for d in range(spaces)], device) for k in range(modes_z)]
            for node, source in enumerate((x_part, y_part)):
                target[node, z] = sum(w * source[pl.ds(k * modes_x, modes_x), :] for k, w in enumerate(weights))


def chain_kernel(count, spaces, pieces, factor, *refs):
    out = refs[-1]
    gain = factor[...] * factor[...]
    state = jnp.zeros_like(gain)
    for t in range(count):
        for s in range(spaces):
            out[t * spaces + s] = state
        if t < count - 1:
            total = pieces[t * spaces]
            for s in range(1, spaces):
                total = total + pieces[t * spaces + s]
            state = gain * state + total


def finish_kernel(spaces, carried, one, two, keep, *refs):
    received = refs[: spaces - 1]
    table_x, table_y, table_f, out, left, right, wide, result, sems = refs[spaces - 1 :]
    planes, modes_x, lanes = keep.shape[1:]
    modes_z = table_f.shape[0] // modes_x
    width_y = out.shape[5]
    me = lax.axis_index("space")
    table = sine_table(planes * spaces, modes_z)
    for k in range(modes_z):
        part = pl.ds(k * modes_x, modes_x)
        left[part, :] = table_f[part, :] * carried[part, :]
        right[part, :] = table_f[part, :] * left[part, :]
    copies = []
    for node, source in ((0, left), (1, right)):
        for z in range(planes):
            value = keep[node, z]
            for other in received:
                value = value + other[node, z]
            for k in range(modes_z):
                weight = pick([table[d * planes + z, k] for d in range(spaces)], me)
                value = value + weight * source[pl.ds(k * modes_x, modes_x), :]
            high, low = split(value)
            wide[node * planes + z] = dot(jnp.concatenate([high, low], axis=1), table_y[0]) + dot(
                high, table_y[1, :lanes]
            )
    for node, swept in ((0, one), (1, two)):
        for z in range(planes):
            high, low = split(wide[node * planes + z])
            fine = dot(table_x[...], jnp.concatenate([high, high, low], axis=0))
            for s in range(2):
                result[node, s, z] = plane(swept, s, z) + fine[:, s * width_y : (s + 1) * width_y]
            copy = pltpu.make_async_copy(result.at[node, :, z], out.at[0, node, :, z], sems.at[node * planes + z])
            copy.start()
            copies.append(copy)
    for copy in copies:
        copy.wait()


def iteration(nodes, initial):
    count, spaces = lax.axis_size("tm"), lax.axis_size("space")
    planes, width_x, width_y = initial.shape[1:]
    modes_x, modes_y, modes_z = width_x // 2, width_y // 2, planes * spaces // 2
    half, lanes = planes // 2, 2 * modes_y
    devices = count * spaces
    f32 = jnp.float32
    shape = jax.ShapeDtypeStruct
    vmem, far = pl.BlockSpec(memory_space=pltpu.VMEM), pl.BlockSpec(memory_space=pltpu.HBM)
    params = pltpu.CompilerParams(vmem_limit_bytes=24 << 20)
    sides = 1 if spaces == 2 else 2
    sem = pltpu.SemaphoreType.DMA

    def in_hbm(value):
        return pltpu.with_memory_space_constraint(jnp.asarray(value), pltpu.HBM)

    nodes, initial = in_hbm(nodes), in_hbm(initial)
    rows = modes_z * modes_x
    share = rows // devices
    factors = factor_table(modes_z, modes_x, modes_y)
    high_x, low_x = np_split(sine_table(width_x, modes_x))
    high_y, low_y = np_split(doubled(sine_table(width_y, modes_y).T))
    tables = [
        factors.reshape(devices, share, lanes),
        np.stack(np_split(restricted(modes_x))),
        np.concatenate(np_split(doubled(restricted(modes_y).T)), axis=1),
        factors,
        np.concatenate([high_x, low_x, high_x], axis=1),
        np.stack([np.concatenate([high_y, high_y]), np.concatenate([low_y, low_y])]),
    ]
    near = [shape((share, lanes), f32)] + [shape(table.shape, table.dtype) for table in tables[1:]]

    plane_pair = shape((2, 2, width_x, width_y), f32)
    whole = shape((2, planes, width_x, width_y), f32)
    rimmed = shape((2, planes, width_x + 2 * RIM, width_y), f32)
    cuts = [2, planes - 2] if spaces == 2 else [planes]
    edge = pl.pallas_call(
        functools.partial(load_kernel, spaces, count),
        out_shape=shape((2, cuts[0], width_x, width_y), f32),
        in_specs=[far, far],
        out_specs=vmem,
        scratch_shapes=[sem((1,))],
        compiler_params=params,
        name="load",
    )(nodes, initial)
    onward = [(t, (t + 1) % count) for t in range(count)]
    parts = [lax.ppermute(edge, "tm", onward)]
    one, rest, *others = pl.pallas_call(
        functools.partial(early_kernel, spaces, count),
        out_shape=[whole] * 2
        + [plane_pair] * sides
        + near
        + [shape((2, cut, width_x, width_y), f32) for cut in cuts[1:]],
        in_specs=[far] * (2 + TABLES),
        out_specs=[vmem] * (2 + sides + TABLES + len(cuts) - 1),
        scratch_shapes=[pltpu.VMEM(rimmed.shape, f32)] * 2 + [sem((3 + TABLES,))],
        compiler_params=params,
        name="early",
    )(nodes, initial, *[in_hbm(table) for table in tables])
    owns, near, inner = others[:sides], others[sides : sides + TABLES], others[sides + TABLES :]
    parts += [lax.ppermute(part, "tm", onward) for part in inner]
    merged = pl.pallas_call(
        functools.partial(merge_kernel, spaces, planes),
        out_shape=[plane_pair] * sides,
        in_specs=[vmem] * (1 + sides),
        out_specs=[vmem] * sides,
        scratch_shapes=[pltpu.VMEM((2, cuts[0], width_x + 2 * RIM, width_y), f32)],
        compiler_params=params,
        name="merge",
    )(parts[0], *owns)
    halos = []
    for n, part in enumerate(merged):
        if spaces == 2:
            moves = [(0, 1), (1, 0)]
        else:
            step = -1 if n == 0 else 1
            moves = [(s, s + step) for s in range(spaces) if 0 <= s + step < spaces]
        halos.append(lax.ppermute(part, "space", moves))
    if spaces != 2:
        halos = halos[::-1]
    start, one, rest, *bases = pl.pallas_call(
        functools.partial(start_kernel, spaces),
        out_shape=[rimmed] + [whole] * 2 + [shape((2, half, width_x, width_y), f32)] * 2,
        in_specs=[vmem] * (len(cuts) + 2),
        out_specs=[vmem] * 5,
        compiler_params=params,
        name="begin",
    )(*parts, one, rest)

    block = shape((2, planes, modes_x, lanes), f32)
    fields = 3 * half + 2 * sides
    one, two, element, keep, *sends = pl.pallas_call(
        functools.partial(sweep_kernel, spaces),
        out_shape=[rimmed] * 2 + [shape((rows, lanes), f32)] + [block] * spaces,
        in_specs=[vmem] * (5 + 2 * sides + 3),
        out_specs=[vmem] * (3 + spaces),
        scratch_shapes=[
            pltpu.VMEM((2, half, width_x, width_y), f32),
            pltpu.VMEM((fields * width_x, 2 * width_y), f32),
            pltpu.VMEM((width_x, fields * lanes), f32),
            pltpu.VMEM((modes_x, fields * lanes), f32),
            pltpu.VMEM((rows, lanes), f32),
            pltpu.VMEM((rows, lanes), f32),
        ],
        compiler_params=params,
        name="sweep",
    )(start, one, rest, *bases, *halos, *owns, *near[1:4])

    received = []
    for j, send in enumerate(sends, 1):
        received.append(lax.ppermute(send, "space", [(s, (s + j) % spaces) for s in range(spaces)]))
    pieces = lax.all_to_all(element.reshape(devices, share, lanes), AXES, 0, 0, tiled=True)
    carried = pl.pallas_call(
        functools.partial(chain_kernel, count, spaces),
        out_shape=shape((devices, share, lanes), f32),
        in_specs=[vmem, vmem] + [pl.BlockSpec(memory_space=pl.ANY)] * (spaces - 1),
        out_specs=vmem,
        compiler_params=params,
        name="chain",
    )(pieces, near[0], *received)
    carried = lax.all_to_all(carried, AXES, 0, 0, tiled=True).reshape(rows, lanes)

    return pl.pallas_call(
        functools.partial(finish_kernel, spaces),
        out_shape=shape((1, 2, 2, planes, width_x, width_y), f32),
        in_specs=[vmem] * (4 + spaces - 1 + 3),
        out_specs=far,
        scratch_shapes=[pltpu.VMEM((rows, lanes), f32)] * 2
        + [
            pltpu.VMEM((2 * planes, modes_x, 2 * width_y), f32),
            pltpu.VMEM((2, 2, planes, width_x, width_y), f32),
            sem((2 * planes,)),
        ],
        compiler_params=params,
        name="finish",
    )(carried, one, two, keep, *received, near[4], near[5], near[3])


def solution(mesh):
    in_specs = (P("tm", None, None, "space", None, None), P(None, "space", None, None))
    out_specs = P("tm", None, None, "space", None, None)
    return jax.shard_map(iteration, mesh=mesh, in_specs=in_specs, out_specs=out_specs, check_vma=False)
```
